256 devices in a mesh: aux: 32 (over z, y), occ: 8 (over x, core).
Axes of the slice: x: 4, y: 4, z: 8, core: 2. Of those that a mesh axis runs over, the one named last changes fastest.
Arguments:
- ints: bfloat16 [32, 16, 16, 16384], P(None, None, None, 'aux'), may hold values from -0.125 to 0.125
- blk_atoms: int32 [1024, 2], P('aux'), may hold values from 0 to 255
- blk_count: int32 [32], P('aux'), may hold values from 1 to 32, as said below
- occ_coeff: bfloat16 [1280, 4096], P(None, 'occ'), may hold values from -1.5 to 1.5
- vir_coeff: bfloat16 [4096, 3072], P(None, 'occ'), may hold values from -1.5 to 1.5
- batch_ids: int32 [8], replicated, may hold values from 0 to 1279, as said below
Outputs:
- pair_ints: float32 [8, 32, 96, 8, 96], P(None, 'aux', 'occ')
The draws below stay inside these ranges and needn't reach their ends.
Inputs may be any that keep to these rules, and one draw needn't show every extreme that they name: `batch_ids`: the batch's orbitals are distinct, and the batch holds the last occupied orbital. `blk_count`: every owner has at least one live slot, and some owner has all 32 live. Slots of owner g name atoms within 2 * 256 // 32 (at least 2) atoms after atom g * 8, cyclically.
All inputs are finite; a program needn't handle non-finite values.
Results may differ from the reference program's by a relative error of at most 0.0017.
Values may be sent and summed in bfloat16 or wider, within the bound.
A program may use at most 128 MiB of HBM per device.

```python
import jax
import jax.numpy as jnp
from jax import lax

BS = 16
NATOM = 256
NOCC = 1280
OB = 8
NBLK = 32
AUX_DEV = 512
AV = 12
NGROUP = 32
NAUX = 16384
GROUP = 96
NV = 3072
NAO = 4096
N_OCC = 8


def draw_blk_atoms(key, part):
    row_total = NGROUP * NBLK
    owner_ids = jnp.arange(row_total, dtype=jnp.int32) // NBLK
    centre_atom = owner_ids * NATOM // NGROUP
    reach_atoms = max(2 * NATOM // NGROUP, 2)
    offsets = jax.random.randint(key, (row_total, 2), 0, reach_atoms, dtype=jnp.int32)
    return ((centre_atom[:, None] + offsets) % NATOM).astype(jnp.int32)


def draw_blk_count(key, part):
    drawn = jax.random.randint(key, (NGROUP,), 1, NBLK + 1, dtype=jnp.int32)
    squared = jnp.maximum(drawn * drawn // NBLK, 1)
    busiest = jax.random.randint(jax.random.fold_in(key, 7), (), 0, NGROUP, dtype=jnp.int32)
    return jnp.where(jnp.arange(NGROUP, dtype=jnp.int32) == busiest, NBLK, squared).astype(jnp.int32)


def draw_batch_ids(key, part):
    inner_ids = jax.random.permutation(key, NOCC - 1)[:OB - 1].astype(jnp.int32)
    end_ids = jnp.array([NOCC - 1], dtype=jnp.int32)
    joined = jnp.concatenate([end_ids, inner_ids])
    shuffle = jax.random.permutation(jax.random.fold_in(key, 3), OB)
    return joined[shuffle].astype(jnp.int32)


def shard_levels(own_key, extent, shards, smallest, top_value):
    def one(dim, shards_of):
        steps = jax.random.uniform(jax.random.fold_in(jax.random.fold_in(own_key, 6), dim), (shards_of,), jnp.float32, smallest / len(shards), top_value / len(shards))
        return jnp.repeat(jnp.exp(steps), extent[dim] // shards_of).reshape((-1,) + (1,) * (len(extent) - dim - 1))

    level = one(*shards[0])
    for cut in shards[1:]:
        level = level * one(*cut)
    return level


def gaussian(own_key, shape, deviation, bound, cuts=(), kind=jnp.bfloat16):
    values = jax.random.normal(own_key, shape, jnp.float32) * deviation
    if len(cuts) > 0:
        values = shard_levels(own_key, shape, cuts, -0.22, 0.18) * values
    return jnp.clip(values, min=-bound, max=bound).astype(kind)


def setup_inputs(seed: int = 0) -> dict:
    arg_keys = jax.random.split(jax.random.key(seed), 7)
    return {
        "ints": gaussian(arg_keys[0], (NBLK, BS, BS, NAUX), (1.5 * (NBLK * NAUX ** 0.5) ** -0.5), 0.125, ((3, 32),)),
        "blk_atoms": draw_blk_atoms(jax.random.fold_in(arg_keys[6], 71), 0),
        "blk_count": draw_blk_count(jax.random.fold_in(arg_keys[6], 71), 0),
        "occ_coeff": gaussian(arg_keys[3], (NOCC, NAO), BS ** -0.5, 1.5, ((1, 8),)),
        "vir_coeff": gaussian(arg_keys[4], (NAO, NV), BS ** -0.5, 1.5, ((1, 8),)),
        "batch_ids": draw_batch_ids(jax.random.fold_in(arg_keys[6], 71), 0),
    }


def reference(ints, blk_atoms, blk_count, occ_coeff, vir_coeff, batch_ids):
    batch_coeff = occ_coeff[batch_ids]
    per_atom = batch_coeff.reshape(OB, NATOM, BS).astype(jnp.float32)
    vir_atoms = vir_coeff.reshape(NATOM, BS, NV).astype(jnp.float32)

    def owner_fitted(owner_index):
        slot_atoms = lax.dynamic_slice_in_dim(blk_atoms, owner_index * NBLK, NBLK, 0)
        owner_ints = lax.dynamic_slice_in_dim(ints, owner_index * AUX_DEV, AUX_DEV, 3).astype(jnp.float32)
        left_rows = per_atom[:, slot_atoms[:, 0], :]
        half_ints = jnp.einsum('ikm,kmnq->kinq', left_rows, owner_ints)
        live_slots = jnp.arange(NBLK, dtype=jnp.int32) < blk_count[owner_index]
        half_ints = jnp.where(live_slots[:, None, None, None], half_ints, 0.0).astype(jnp.bfloat16)
        half_ints = lax.optimization_barrier(half_ints).astype(jnp.float32)
        right_rows = vir_atoms[slot_atoms[:, 1]]
        return jnp.einsum('knv,kinq->ivq', right_rows, half_ints).astype(jnp.bfloat16)

    fitted = lax.map(owner_fitted, jnp.arange(NGROUP, dtype=jnp.int32))
    arranged = fitted.reshape(NGROUP, OB, N_OCC, NGROUP, AV, AUX_DEV)

    def group_pairs(group_index):
        group_rows = lax.dynamic_index_in_dim(arranged, group_index, 3, keepdims=False)
        group_rows = jnp.transpose(group_rows, (1, 2, 3, 0, 4)).reshape(OB, GROUP, NAUX).astype(jnp.float32)
        return jnp.einsum('icq,jdq->icjd', group_rows, group_rows)

    pair_ints = lax.map(group_pairs, jnp.arange(NGROUP, dtype=jnp.int32))
    return jnp.transpose(pair_ints, (1, 0, 2, 3, 4))
```

```python
import jax
import jax.numpy as jnp
from jax import lax
from jax.experimental import pallas as pl
from jax.experimental.pallas import tpu as pltpu
from jax.sharding import PartitionSpec as P

ROWS = 4


def fit_kernel(vir_ref, half_ref, place_ref, fit_ref):
    ranks = vir_ref.shape[0]
    wide = jnp.concatenate([vir_ref[a] for a in range(ranks)], axis=1)
    placed = jnp.dot(wide, place_ref[...], preferred_element_type=jnp.float32).astype(jnp.bfloat16)
    groups, owners, width = fit_ref.shape[0], fit_ref.shape[1], fit_ref.shape[2]
    span = groups * width
    for t in range(owners):
        summed = lax.dot_general(
            placed[:, span * t : span * (t + 1)],
            half_ref[t],
            (((0,), (0,)), ((), ())),
            preferred_element_type=jnp.float32,
        )
        for g in range(groups):
            fit_ref[g, t] = summed[width * g : width * (g + 1)].astype(jnp.bfloat16)


def gram_kernel(fit_ref, out_ref, rows, gram, sorted_rows):
    owners, width, lanes = fit_ref.shape
    batch = rows.shape[0] // width
    part = lanes // batch
    for o in range(owners // 2):
        for h in range(batch // 2):
            first = fit_ref[2 * o, :, 2 * part * h : 2 * part * (h + 1)]
            second = fit_ref[2 * o + 1, :, 2 * part * h : 2 * part * (h + 1)]
            cols = slice(2 * part * o, 2 * part * (o + 1))
            rows[width * 2 * h : width * (2 * h + 1), cols] = jnp.concatenate(
                [first[:, :part], second[:, :part]], axis=1
            )
            rows[width * (2 * h + 1) : width * (2 * h + 2), cols] = jnp.concatenate(
                [first[:, part:], second[:, part:]], axis=1
            )
    half = rows.shape[0] // 2
    for t in range(2):
        gram[half * t : half * (t + 1)] = lax.dot_general(
            rows[half * t : half * (t + 1)],
            rows[...],
            (((1,), (1,)), ((), ())),
            preferred_element_type=jnp.float32,
        )
    ranks = out_ref.shape[0]
    kept = width // ranks
    for a in range(ranks):
        for i in range(batch):
            sorted_rows[kept * i : kept * (i + 1)] = gram[
                width * i + kept * a : width * i + kept * (a + 1)
            ]
        out_ref[a] = sorted_rows[...].astype(jnp.bfloat16)


def on_device(ints, blk_atoms, blk_count, occ_coeff, vir_coeff, batch_ids):
    batch = batch_ids.shape[0]
    slots, block_size = ints.shape[0], ints.shape[1]
    aux_local = ints.shape[3]
    ranks = lax.axis_size("occ")
    group_count = lax.axis_size("aux")
    planes = group_count // ROWS
    owner, rank = lax.axis_index("aux"), lax.axis_index("occ")
    plane, row = owner // ROWS, owner % ROWS
    atom_total = vir_coeff.shape[0] // block_size
    step = atom_total // group_count
    window = 2 * step + 1
    depth = window * block_size
    part = aux_local // ranks
    vir_group = vir_coeff.shape[1] // group_count
    width = vir_group * ranks
    lane = 64

    with jax.named_scope("vir_rows"):
        cols = lax.dynamic_slice_in_dim(vir_coeff, plane * (ROWS * vir_group), ROWS * vir_group, 1)
        cols = jnp.pad(cols, ((0, 0), (0, lane - ROWS * vir_group)))
        stride = ROWS * step * block_size
        reach = stride * (planes - 1) + depth
        start = row * (step * block_size)
        longest = (ROWS - 1) * step * block_size + reach
        cols = jnp.concatenate([cols, cols[: longest - cols.shape[0]]], axis=0)
        cols = lax.dynamic_slice_in_dim(cols, start, reach, 0)
        vir_rows = jnp.concatenate(
            [cols[stride * z : stride * z + depth] for z in range(planes)], axis=1
        )
        vir_all = lax.all_gather(vir_rows, "occ", axis=0)

    with jax.named_scope("half"):
        picked = jnp.take(occ_coeff, batch_ids, axis=0)
        batch_coeff = lax.all_gather(picked, "occ", axis=1, tiled=True)
        left = batch_coeff.reshape(batch, atom_total, block_size)[:, blk_atoms[:, 0], :]
        left = left.reshape(batch, slots * block_size)
        offset = (blk_atoms[:, 1] - owner * step + atom_total) % atom_total
        offset = jnp.where(jnp.arange(slots, dtype=jnp.int32) < blk_count[0], offset, -1)
        offset = jnp.repeat(offset, block_size)
        hits = offset[None, :] == jnp.arange(window, dtype=jnp.int32)[:, None]
        spread = jnp.where(hits[:, None, :], left[None], jnp.bfloat16(0))
        mine = lax.dynamic_slice_in_dim(ints, rank * part, part, 3)
        half = jnp.einsum(
            "wik,knq->wniq",
            spread,
            mine.reshape(slots * block_size, block_size, part),
            preferred_element_type=jnp.float32,
        ).astype(jnp.bfloat16)
        half = half.reshape(depth, batch * part)
        along_z = [[z * ROWS + y for z in range(planes)] for y in range(ROWS)]
        half_all = lax.all_gather(half, "aux", axis=0, axis_index_groups=along_z)

    with jax.named_scope("fit"):
        source = jnp.arange(ranks * 2 * lane, dtype=jnp.int32)[:, None]
        target = jnp.arange(2 * ROWS * width, dtype=jnp.int32)[None, :]
        wanted = (
            (target // vir_group % ranks) * (2 * lane)
            + (target // (ROWS * width)) * lane
            + (target // width % ROWS) * vir_group
            + target % vir_group
        )
        place = (source == wanted).astype(jnp.bfloat16)
        fitted = pl.pallas_call(
            fit_kernel,
            grid=(planes // 2,),
            in_specs=[
                pl.BlockSpec((ranks, depth, 2 * lane), lambda s: (0, 0, s)),
                pl.BlockSpec((2, depth, batch * part), lambda s: (s, 0, 0)),
                pl.BlockSpec(place.shape, lambda s: (0, 0)),
            ],
            out_specs=pl.BlockSpec((ROWS, 2, width, batch * part), lambda s: (0, s, 0, 0)),
            out_shape=jax.ShapeDtypeStruct((ROWS, planes, width, batch * part), jnp.bfloat16),
        )(vir_all, half_all, place)
        along_y = [[z * ROWS + y for y in range(ROWS)] for z in range(planes)]
        regrouped = lax.all_to_all(
            fitted, "aux", split_axis=0, concat_axis=0, axis_index_groups=along_y, tiled=True
        )

    with jax.named_scope("gram"):
        total = batch * width
        kept = total // ranks
        partial = pl.pallas_call(
            gram_kernel,
            out_shape=jax.ShapeDtypeStruct((ranks, kept, total), jnp.bfloat16),
            in_specs=[pl.BlockSpec(memory_space=pltpu.VMEM)],
            out_specs=pl.BlockSpec(memory_space=pltpu.VMEM),
            scratch_shapes=[
                pltpu.VMEM((total, group_count * part), jnp.bfloat16),
                pltpu.VMEM((total, total), jnp.float32),
                pltpu.VMEM((kept, total), jnp.float32),
            ],
        )(regrouped.reshape(group_count, width, batch * part))
        shares = lax.all_to_all(partial, "occ", split_axis=0, concat_axis=0, tiled=True)
        pair_ints = jnp.sum(shares.astype(jnp.float32), axis=0)
        return pair_ints.reshape(batch, 1, vir_group, batch, width)


def solution(mesh):
    in_specs = (
        P(None, None, None, "aux"),
        P("aux", None),
        P("aux"),
        P(None, "occ"),
        P(None, "occ"),
        P(),
    )
    out_specs = P(None, "aux", "occ", None, None)
    return jax.shard_map(
        on_device, mesh=mesh, in_specs=in_specs, out_specs=out_specs, check_vma=False
    )
```

```python
import jax
import jax.numpy as jnp
from jax import lax
from jax.experimental import pallas as pl
from jax.experimental.pallas import tpu as pltpu
from jax.sharding import PartitionSpec as P

ROWS = 4


def exchange_kernel(
    vir_ref, half_ref, place_ref, out_ref,
    held, own, stage, relay, arrived, rows, gram, sorted_rows,
    ring_send, ring_recv, step_send, step_recv, pass_send, pass_recv,
):
    owner, rank = lax.axis_index("aux"), lax.axis_index("occ")
    plane, row = owner // ROWS, owner % ROWS
    blocks = own.shape[0]
    above, below = lax.rem(plane + 1, blocks) * ROWS + row, lax.rem(plane + blocks - 1, blocks) * ROWS + row
    after = plane * ROWS + lax.rem(row + 1, ROWS)
    before = plane * ROWS + lax.rem(row + ROWS - 1, ROWS)
    ranks = vir_ref.shape[0]
    width, lanes = own.shape[1], own.shape[2]
    batch = gram.shape[0] // width
    part = lanes // batch
    span = ROWS * width

    barrier = pltpu.get_barrier_semaphore()
    for peer in (above, below, after, before):
        pl.semaphore_signal(
            barrier, inc=1, device_id=(peer, rank), device_id_type=pl.DeviceIdType.MESH
        )
    pl.semaphore_wait(barrier, 4)

    def send(source, target, send_sem, recv_sem, peer):
        copy = pltpu.make_async_remote_copy(
            src_ref=source,
            dst_ref=target,
            send_sem=send_sem,
            recv_sem=recv_sem,
            device_id=(peer, rank),
            device_id_type=pl.DeviceIdType.MESH,
        )
        copy.start()
        return copy

    ring, direct, passed = {}, {}, {}

    def send_ring(b, source):
        ring[b] = send(
            source, held.at[b - 1], ring_send.at[b - 1], ring_recv.at[b - 1],
            above if b % 2 else below,
        )

    def pass_on(b):
        direct[b, 2].wait_recv()
        passed[b] = send(
            relay.at[b], arrived.at[1, b], pass_send.at[b], pass_recv.at[b],
            before if b % 2 else after,
        )

    def accumulate(p):
        first, second = 2 * p, 2 * p + 1
        for b in (first, second):
            direct[b, 1].wait_recv()
            direct[b, 3].wait_recv()
            passed[b].wait_recv()
        for r in range(ROWS):
            for h in range(batch // 2):
                cols = slice(2 * part * h, 2 * part * (h + 1))
                if r == 0:
                    one, two = own[first, :, cols], own[second, :, cols]
                else:
                    one, two = arrived[r - 1, first, :, cols], arrived[r - 1, second, :, cols]
                place = slice(2 * part * r, 2 * part * (r + 1))
                rows[width * 2 * h : width * (2 * h + 1), place] = jnp.concatenate(
                    [one[:, :part], two[:, :part]], axis=1
                )
                rows[width * (2 * h + 1) : width * (2 * h + 2), place] = jnp.concatenate(
                    [one[:, part:], two[:, part:]], axis=1
                )
        half = rows.shape[0] // 2
        for t in range(2):
            product = lax.dot_general(
                rows[half * t : half * (t + 1)],
                rows[...],
                (((1,), (1,)), ((), ())),
                preferred_element_type=jnp.float32,
            )
            if p == 0:
                gram[half * t : half * (t + 1)] = product
            else:
                gram[half * t : half * (t + 1)] += product

    send_ring(1, half_ref)
    send_ring(2, half_ref)
    for b in range(blocks):
        if b > 0:
            ring[b].wait_recv()
            if b + 2 < blocks:
                send_ring(b + 2, held.at[b - 1])
        if b % 2 == 0:
            wide = jnp.concatenate(
                [vir_ref[a, :, 64 * b : 64 * (b + 2)] for a in range(ranks)], axis=1
            )
            placed = jnp.dot(
                wide, place_ref[...], preferred_element_type=jnp.float32
            ).astype(jnp.bfloat16)
        t = b % 2
        summed = lax.dot_general(
            placed[:, span * t : span * (t + 1)],
            half_ref[...] if b == 0 else held[b - 1],
            (((0,), (0,)), ((), ())),
            preferred_element_type=jnp.float32,
        ).astype(jnp.bfloat16)
        own[b] = summed[:width]
        for r in range(1, ROWS):
            stage[b, r - 1] = summed[width * r : width * (r + 1)]
        direct[b, 1] = send(
            stage.at[b, 0], arrived.at[0, b], step_send.at[b, 0], step_recv.at[b, 0], after
        )
        direct[b, 3] = send(
            stage.at[b, 2], arrived.at[2, b], step_send.at[b, 2], step_recv.at[b, 2], before
        )
        direct[b, 2] = send(
            stage.at[b, 1], relay.at[b], step_send.at[b, 1], step_recv.at[b, 1],
            before if b % 2 else after,
        )
        if b > 0:
            pass_on(b - 1)
        if b % 2 and b > 2:
            accumulate((b - 3) // 2)
    pass_on(blocks - 1)
    accumulate(blocks // 2 - 1)
    for copy in [*ring.values(), *direct.values(), *passed.values()]:
        copy.wait_send()

    kept = width // ranks
    for a in range(ranks):
        for i in range(batch):
            sorted_rows[kept * i : kept * (i + 1)] = gram[
                width * i + kept * a : width * i + kept * (a + 1)
            ]
        out_ref[a] = sorted_rows[...].astype(jnp.bfloat16)


def ring_order(count):
    order = [0]
    for k in range(1, count // 2 + 1):
        order += [-k, k]
    return order[:count]


def on_device(ints, blk_atoms, blk_count, occ_coeff, vir_coeff, batch_ids):
    batch = batch_ids.shape[0]
    slots, block_size = ints.shape[0], ints.shape[1]
    aux_local = ints.shape[3]
    ranks = lax.axis_size("occ")
    group_count = lax.axis_size("aux")
    planes = group_count // ROWS
    owner, rank = lax.axis_index("aux"), lax.axis_index("occ")
    plane, row = owner // ROWS, owner % ROWS
    atom_total = vir_coeff.shape[0] // block_size
    step = atom_total // group_count
    window = 2 * step + 1
    depth = window * block_size
    part = aux_local // ranks
    vir_group = vir_coeff.shape[1] // group_count
    width = vir_group * ranks
    lane = 64

    with jax.named_scope("vir_rows"):
        cols = lax.dynamic_slice_in_dim(vir_coeff, plane * (ROWS * vir_group), ROWS * vir_group, 1)
        cols = jnp.pad(cols, ((0, 0), (0, lane - ROWS * vir_group)))
        cols = jnp.concatenate([cols, cols[:depth]], axis=0)
        pieces = []
        for shift in ring_order(planes):
            source = ((plane + shift + planes) % planes) * ROWS + row
            pieces.append(lax.dynamic_slice_in_dim(cols, source * (step * block_size), depth, 0))
        vir_rows = jnp.concatenate(pieces, axis=1)
        vir_all = lax.all_gather(vir_rows, "occ", axis=0)

    with jax.named_scope("half"):
        picked = jnp.take(occ_coeff, batch_ids, axis=0)
        batch_coeff = lax.all_gather(picked, "occ", axis=1, tiled=True)
        left = batch_coeff.reshape(batch, atom_total, block_size)[:, blk_atoms[:, 0], :]
        left = left.reshape(batch, slots * block_size)
        offset = (blk_atoms[:, 1] - owner * step + atom_total) % atom_total
        offset = jnp.where(jnp.arange(slots, dtype=jnp.int32) < blk_count[0], offset, -1)
        offset = jnp.repeat(offset, block_size)
        hits = offset[None, :] == jnp.arange(window, dtype=jnp.int32)[:, None]
        spread = jnp.where(hits[:, None, :], left[None], jnp.bfloat16(0))
        mine = lax.dynamic_slice_in_dim(ints, rank * part, part, 3)
        half = jnp.einsum(
            "wik,knq->wniq",
            spread,
            mine.reshape(slots * block_size, block_size, part),
            preferred_element_type=jnp.float32,
        ).astype(jnp.bfloat16)
        half = half.reshape(depth, batch * part)

    with jax.named_scope("fit"):
        source = jnp.arange(ranks * 2 * lane, dtype=jnp.int32)[:, None]
        target = jnp.arange(2 * ROWS * width, dtype=jnp.int32)[None, :]
        wanted = (
            (target // vir_group % ranks) * (2 * lane)
            + (target // (ROWS * width)) * lane
            + ((target // width + row) % ROWS) * vir_group
            + target % vir_group
        )
        place = (source == wanted).astype(jnp.bfloat16)
        total = batch * width
        kept = total // ranks
        piece = (width, batch * part)
        dma = pltpu.SemaphoreType.DMA
        partial = pl.pallas_call(
            exchange_kernel,
            out_shape=jax.ShapeDtypeStruct((ranks, kept, total), jnp.bfloat16),
            in_specs=[pl.BlockSpec(memory_space=pltpu.VMEM)] * 3,
            out_specs=pl.BlockSpec(memory_space=pltpu.VMEM),
            scratch_shapes=[
                pltpu.VMEM((planes - 1, depth, batch * part), jnp.bfloat16),
                pltpu.VMEM((planes, *piece), jnp.bfloat16),
                pltpu.VMEM((planes, ROWS - 1, *piece), jnp.bfloat16),
                pltpu.VMEM((planes, *piece), jnp.bfloat16),
                pltpu.VMEM((ROWS - 1, planes, *piece), jnp.bfloat16),
                pltpu.VMEM((total, ROWS * 2 * part), jnp.bfloat16),
                pltpu.VMEM((total, total), jnp.float32),
                pltpu.VMEM((kept, total), jnp.float32),
                dma((planes - 1,)),
                dma((planes - 1,)),
                dma((planes, ROWS - 1)),
                dma((planes, ROWS - 1)),
                dma((planes,)),
                dma((planes,)),
            ],
            compiler_params=pltpu.CompilerParams(collective_id=0, has_side_effects=True),
        )(vir_all, half, place)

    with jax.named_scope("pairs"):
        shares = lax.all_to_all(partial, "occ", split_axis=0, concat_axis=0, tiled=True)
        pair_ints = jnp.sum(shares.astype(jnp.float32), axis=0)
        return pair_ints.reshape(batch, 1, vir_group, batch, width)


def solution(mesh):
    in_specs = (
        P(None, None, None, "aux"),
        P("aux", None),
        P("aux"),
        P(None, "occ"),
        P(None, "occ"),
        P(),
    )
    out_specs = P(None, "aux", "occ", None, None)
    return jax.shard_map(
        on_device, mesh=mesh, in_specs=in_specs, out_specs=out_specs, check_vma=False
    )
```

```python
import jax
import jax.numpy as jnp
from jax import lax
from jax.experimental import pallas as pl
from jax.experimental.pallas import tpu as pltpu
from jax.sharding import PartitionSpec as P

ROWS = 4


def exchange_kernel(
    vir_ref, half_ref, place_ref, out_ref,
    vir_held, held, own, stage, relay, arrived, rows, gram, sorted_rows,
    joined, mine, others,
    vir_send, vir_recv, ring_send, ring_recv, step_send, step_recv, pass_send, pass_recv,
    join_send, join_recv, sum_send, sum_recv,
):
    owner, rank = lax.axis_index("aux"), lax.axis_index("occ")
    plane, row = owner // ROWS, owner % ROWS
    blocks = own.shape[0]
    above, below = lax.rem(plane + 1, blocks) * ROWS + row, lax.rem(plane + blocks - 1, blocks) * ROWS + row
    after = plane * ROWS + lax.rem(row + 1, ROWS)
    before = plane * ROWS + lax.rem(row + ROWS - 1, ROWS)
    parts, ranks = vir_ref.shape[0], vir_held.shape[1] + 1
    chips = ranks // 2
    core = lax.rem(rank, 2)
    partner = rank + 1 - 2 * core
    width, lanes = own.shape[1], own.shape[2]
    batch = gram.shape[0] // width
    part = lanes // batch
    span = ROWS * width

    barrier = pltpu.get_barrier_semaphore()
    near = [(peer, rank) for peer in (above, below, after, before)]
    near += [(owner, partner)] + [(owner, lax.rem(rank + 2 * k, ranks)) for k in range(1, chips)]
    for peer in near:
        pl.semaphore_signal(barrier, inc=1, device_id=peer, device_id_type=pl.DeviceIdType.MESH)
    pl.semaphore_wait(barrier, len(near))

    def send(source, target, send_sem, recv_sem, peer, peer_rank=rank):
        copy = pltpu.make_async_remote_copy(
            src_ref=source,
            dst_ref=target,
            send_sem=send_sem,
            recv_sem=recv_sem,
            device_id=(peer, peer_rank),
            device_id_type=pl.DeviceIdType.MESH,
        )
        copy.start()
        return copy

    ring, direct, passed, spread, joins, sums = {}, {}, {}, {}, {}, {}

    def send_vir(p, k, d, source, peer_rank):
        j = 2 * k + d - 1
        spread[p, j] = send(
            source, vir_held.at[p, j], vir_send.at[p, j], vir_recv.at[p, j], owner, peer_rank
        )

    def pass_vir(p):
        for k in range(1, chips):
            spread[p, 2 * k - 1].wait_recv()
            send_vir(p, k, 1, vir_held.at[p, 2 * k - 1], partner)

    def send_ring(b, source):
        ring[b] = send(
            source, held.at[b - 1], ring_send.at[b - 1], ring_recv.at[b - 1],
            above if b % 2 else below,
        )

    def pass_on(b):
        direct[b, 2].wait_recv()
        passed[b] = send(
            relay.at[b], arrived.at[1, b], pass_send.at[b], pass_recv.at[b],
            before if b % 2 else after,
        )

    def accumulate(p):
        first, second = 2 * p, 2 * p + 1
        for b in (first, second):
            direct[b, 1].wait_recv()
            direct[b, 3].wait_recv()
            passed[b].wait_recv()
        for r in range(ROWS):
            for h in range(batch // 2):
                cols = slice(2 * part * h, 2 * part * (h + 1))
                if r == 0:
                    one, two = own[first, :, cols], own[second, :, cols]
                else:
                    one, two = arrived[r - 1, first, :, cols], arrived[r - 1, second, :, cols]
                place = slice(2 * part * r, 2 * part * (r + 1))
                rows[width * 2 * h : width * (2 * h + 1), place] = jnp.concatenate(
                    [one[:, :part], two[:, :part]], axis=1
                )
                rows[width * (2 * h + 1) : width * (2 * h + 2), place] = jnp.concatenate(
                    [one[:, part:], two[:, part:]], axis=1
                )
        half = rows.shape[0] // 2
        for t in range(2):
            product = lax.dot_general(
                rows[half * t : half * (t + 1)],
                rows[...],
                (((1,), (1,)), ((), ())),
                preferred_element_type=jnp.float32,
            )
            if p == 0:
                gram[half * t : half * (t + 1)] = product
            else:
                gram[half * t : half * (t + 1)] += product

    send_ring(1, half_ref)
    send_ring(2, half_ref)
    for p in range(parts):
        for k in range(1, chips):
            send_vir(p, k, 0, vir_ref.at[p], lax.rem(rank + 2 * k, ranks))
        send_vir(p, 0, 1, vir_ref.at[p], partner)
    pass_vir(0)
    for b in range(blocks):
        if b > 0:
            ring[b].wait_recv()
            if b + 2 < blocks:
                send_ring(b + 2, held.at[b - 1])
        if b % 2 == 0:
            p = b // 2
            for k in range(chips):
                spread[p, 2 * k].wait_recv()
            wide = jnp.concatenate(
                [vir_ref[p]] + [vir_held[p, j] for j in range(ranks - 1)], axis=1
            )
            placed = jnp.dot(
                wide, place_ref[...], preferred_element_type=jnp.float32
            ).astype(jnp.bfloat16)
        t = b % 2
        summed = lax.dot_general(
            placed[:, span * t : span * (t + 1)],
            half_ref[...] if b == 0 else held[b - 1],
            (((0,), (0,)), ((), ())),
            preferred_element_type=jnp.float32,
        ).astype(jnp.bfloat16)
        own[b] = summed[:width]
        for r in range(1, ROWS):
            stage[b, r - 1] = summed[width * r : width * (r + 1)]
        direct[b, 1] = send(
            stage.at[b, 0], arrived.at[0, b], step_send.at[b, 0], step_recv.at[b, 0], after
        )
        direct[b, 3] = send(
            stage.at[b, 2], arrived.at[2, b], step_send.at[b, 2], step_recv.at[b, 2], before
        )
        direct[b, 2] = send(
            stage.at[b, 1], relay.at[b], step_send.at[b, 1], step_recv.at[b, 1],
            before if b % 2 else after,
        )
        if b > 0:
            pass_on(b - 1)
        if b % 2 and (b + 1) // 2 < parts:
            pass_vir((b + 1) // 2)
        if b % 2 and b > 2:
            accumulate((b - 3) // 2)
    pass_on(blocks - 1)
    accumulate(blocks // 2 - 1)

    kept = width // ranks
    for a in range(ranks):
        for i in range(batch):
            sorted_rows[a, kept * i : kept * (i + 1)] = gram[
                width * i + kept * a : width * i + kept * (a + 1)
            ]
    chip = rank // 2
    order = [*range(1, chips), 0]
    for k in order:
        theirs = 2 * lax.rem(chip + k, chips) + 1 - core
        joins[k] = send(
            sorted_rows.at[theirs], joined.at[k], join_send.at[k], join_recv.at[k], owner, partner
        )
    for k in order:
        joins[k].wait_recv()
        both = sorted_rows[2 * lax.rem(chip + k, chips) + core] + joined[k]
        if k > 0:
            mine[k - 1] = both.astype(jnp.bfloat16)
            sums[k] = send(
                mine.at[k - 1], others.at[k - 1], sum_send.at[k - 1], sum_recv.at[k - 1],
                owner, lax.rem(rank + 2 * k, ranks),
            )
    for k in range(1, chips):
        sums[k].wait_recv()
        both += others[k - 1].astype(jnp.float32)
    out_ref[...] = both
    for group in (spread, ring, direct, passed, joins, sums):
        for copy in group.values():
            copy.wait_send()


def pick_kernel(mine_ref, index_ref, left_ref, held, send_sem, recv_sem):
    owner, rank = lax.axis_index("aux"), lax.axis_index("occ")
    ranks = held.shape[0]
    barrier = pltpu.get_barrier_semaphore()
    peers = [(owner, lax.rem(rank + r, ranks)) for r in range(1, ranks)]
    for peer in peers:
        pl.semaphore_signal(barrier, inc=1, device_id=peer, device_id_type=pl.DeviceIdType.MESH)
    pl.semaphore_wait(barrier, ranks - 1)
    copies = []
    for r in range(1, ranks):
        copy = pltpu.make_async_remote_copy(
            src_ref=mine_ref,
            dst_ref=held.at[r],
            send_sem=send_sem.at[r],
            recv_sem=recv_sem.at[r],
            device_id=peers[r - 1],
            device_id_type=pl.DeviceIdType.MESH,
        )
        copy.start()
        copies.append(copy)
    span = mine_ref.shape[1]
    column = lax.broadcasted_iota(jnp.int32, (span, index_ref.shape[1]), 0)
    total = None
    for r in range(ranks):
        if r > 0:
            copies[r - 1].wait_recv()
        first = lax.rem(rank + ranks - r, ranks) * span
        hits = jnp.where(column == index_ref[...] - first, 1.0, 0.0).astype(jnp.bfloat16)
        term = jnp.dot(
            mine_ref[...] if r == 0 else held[r], hits, preferred_element_type=jnp.float32
        )
        total = term if total is None else total + term
    left_ref[...] = total.astype(jnp.bfloat16)
    for copy in copies:
        copy.wait_send()


def ring_order(count):
    order = [0]
    for k in range(1, count // 2 + 1):
        order += [-k, k]
    return order[:count]


def slot_of(source, rank, ranks):
    chips = ranks // 2
    return 2 * ((rank // 2 - source // 2 + chips) % chips) + (source + rank) % 2


def on_device(ints, blk_atoms, blk_count, occ_coeff, vir_coeff, batch_ids):
    batch = batch_ids.shape[0]
    slots, block_size = ints.shape[0], ints.shape[1]
    aux_local = ints.shape[3]
    ranks = lax.axis_size("occ")
    group_count = lax.axis_size("aux")
    planes = group_count // ROWS
    owner, rank = lax.axis_index("aux"), lax.axis_index("occ")
    plane, row = owner // ROWS, owner % ROWS
    atom_total = vir_coeff.shape[0] // block_size
    step = atom_total // group_count
    window = 2 * step + 1
    depth = window * block_size
    part = aux_local // ranks
    vir_group = vir_coeff.shape[1] // group_count
    width = vir_group * ranks
    lane = 64

    with jax.named_scope("vir_rows"):
        cols = lax.dynamic_slice_in_dim(vir_coeff, plane * (ROWS * vir_group), ROWS * vir_group, 1)
        cols = jnp.pad(cols, ((0, 0), (0, lane - ROWS * vir_group)))
        cols = jnp.concatenate([cols, cols[:depth]], axis=0)
        pieces = []
        for shift in ring_order(planes):
            source = ((plane + shift + planes) % planes) * ROWS + row
            pieces.append(lax.dynamic_slice_in_dim(cols, source * (step * block_size), depth, 0))
        vir_rows = jnp.stack(
            [jnp.concatenate(pieces[b : b + 2], axis=1) for b in range(0, planes, 2)]
        )

    with jax.named_scope("half"):
        picked = jnp.take(occ_coeff, batch_ids, axis=0)
        index = blk_atoms[:, 0, None] * block_size + jnp.arange(block_size, dtype=jnp.int32)
        vmem = pl.BlockSpec(memory_space=pltpu.VMEM)
        dma = pltpu.SemaphoreType.DMA
        left = pl.pallas_call(
            pick_kernel,
            out_shape=jax.ShapeDtypeStruct((batch, slots * block_size), jnp.bfloat16),
            in_specs=[vmem] * 2,
            out_specs=vmem,
            scratch_shapes=[
                pltpu.VMEM((ranks, *picked.shape), jnp.bfloat16),
                dma((ranks,)),
                dma((ranks,)),
            ],
            compiler_params=pltpu.CompilerParams(collective_id=1, has_side_effects=True),
        )(picked, index.reshape(1, slots * block_size))
        offset = (blk_atoms[:, 1] - owner * step + atom_total) % atom_total
        offset = jnp.where(jnp.arange(slots, dtype=jnp.int32) < blk_count[0], offset, -1)
        offset = jnp.repeat(offset, block_size)
        hits = offset[None, :] == jnp.arange(window, dtype=jnp.int32)[:, None]
        spread = jnp.where(hits[:, None, :], left[None], jnp.bfloat16(0))
        mine = lax.dynamic_slice_in_dim(ints, rank * part, part, 3)
        half = jnp.einsum(
            "wik,knq->wniq",
            spread,
            mine.reshape(slots * block_size, block_size, part),
            preferred_element_type=jnp.float32,
        ).astype(jnp.bfloat16)
        half = half.reshape(depth, batch * part)

    with jax.named_scope("fit"):
        source = jnp.arange(ranks * 2 * lane, dtype=jnp.int32)[:, None]
        target = jnp.arange(2 * ROWS * width, dtype=jnp.int32)[None, :]
        wanted = (
            slot_of(target // vir_group % ranks, rank, ranks) * (2 * lane)
            + (target // (ROWS * width)) * lane
            + ((target // width + row) % ROWS) * vir_group
            + target % vir_group
        )
        place = (source == wanted).astype(jnp.bfloat16)
        total = batch * width
        kept = total // ranks
        piece = (width, batch * part)
        chips = ranks // 2
        pair_ints = pl.pallas_call(
            exchange_kernel,
            out_shape=jax.ShapeDtypeStruct((kept, total), jnp.float32),
            in_specs=[vmem] * 3,
            out_specs=vmem,
            scratch_shapes=[
                pltpu.VMEM((planes // 2, ranks - 1, depth, 2 * lane), jnp.bfloat16),
                pltpu.VMEM((planes - 1, depth, batch * part), jnp.bfloat16),
                pltpu.VMEM((planes, *piece), jnp.bfloat16),
                pltpu.VMEM((planes, ROWS - 1, *piece), jnp.bfloat16),
                pltpu.VMEM((planes, *piece), jnp.bfloat16),
                pltpu.VMEM((ROWS - 1, planes, *piece), jnp.bfloat16),
                pltpu.VMEM((total, ROWS * 2 * part), jnp.bfloat16),
                pltpu.VMEM((total, total), jnp.float32),
                pltpu.VMEM((ranks, kept, total), jnp.float32),
                pltpu.VMEM((chips, kept, total), jnp.float32),
                pltpu.VMEM((chips - 1, kept, total), jnp.bfloat16),
                pltpu.VMEM((chips - 1, kept, total), jnp.bfloat16),
                dma((planes // 2, ranks - 1)),
                dma((planes // 2, ranks - 1)),
                dma((planes - 1,)),
                dma((planes - 1,)),
                dma((planes, ROWS - 1)),
                dma((planes, ROWS - 1)),
                dma((planes,)),
                dma((planes,)),
                dma((chips,)),
                dma((chips,)),
                dma((chips - 1,)),
                dma((chips - 1,)),
            ],
            compiler_params=pltpu.CompilerParams(collective_id=0, has_side_effects=True),
        )(vir_rows, half, place)
        return pair_ints.reshape(batch, 1, vir_group, batch, width)


def solution(mesh):
    in_specs = (
        P(None, None, None, "aux"),
        P("aux", None),
        P("aux"),
        P(None, "occ"),
        P(None, "occ"),
        P(),
    )
    out_specs = P(None, "aux", "occ", None, None)
    return jax.shard_map(
        on_device, mesh=mesh, in_specs=in_specs, out_specs=out_specs, check_vma=False
    )
```

```python
import jax
import jax.numpy as jnp
from jax import lax
from jax.experimental import pallas as pl
from jax.experimental.pallas import tpu as pltpu
from jax.sharding import PartitionSpec as P

ROWS = 4


def exchange_kernel(
    vir_ref, half_ref, place_ref, out_ref,
    vir_held, held, own, stage, relay, arrived, rows, gram, sorted_rows,
    joined, mine, others,
    vir_send, vir_recv, ring_send, ring_recv, step_send, step_recv, pass_send, pass_recv,
    join_send, join_recv, sum_send, sum_recv,
):
    owner, rank = lax.axis_index("aux"), lax.axis_index("occ")
    plane, row = owner // ROWS, owner % ROWS
    blocks = own.shape[0]
    above, below = lax.rem(plane + 1, blocks) * ROWS + row, lax.rem(plane + blocks - 1, blocks) * ROWS + row
    after = plane * ROWS + lax.rem(row + 1, ROWS)
    before = plane * ROWS + lax.rem(row + ROWS - 1, ROWS)
    parts, ranks = vir_ref.shape[0], vir_held.shape[1] + 1
    chips = ranks // 2
    core = lax.rem(rank, 2)
    partner = rank + 1 - 2 * core
    width, lanes = own.shape[1], own.shape[2]
    batch = gram.shape[0] // width
    part = lanes // batch
    span = ROWS * width

    barrier = pltpu.get_barrier_semaphore()
    near = [(peer, rank) for peer in (above, below, after, before)]
    near += [(owner, partner)] + [(owner, lax.rem(rank + 2 * k, ranks)) for k in range(1, chips)]
    for peer in near:
        pl.semaphore_signal(barrier, inc=1, device_id=peer, device_id_type=pl.DeviceIdType.MESH)
    pl.semaphore_wait(barrier, len(near))

    def send(source, target, send_sem, recv_sem, peer, peer_rank=rank):
        copy = pltpu.make_async_remote_copy(
            src_ref=source,
            dst_ref=target,
            send_sem=send_sem,
            recv_sem=recv_sem,
            device_id=(peer, peer_rank),
            device_id_type=pl.DeviceIdType.MESH,
        )
        copy.start()
        return copy

    ring, direct, passed, spread, joins, sums = {}, {}, {}, {}, {}, {}

    def send_vir(p, k, d, source, peer_rank):
        j = 2 * k + d - 1
        spread[p, j] = send(
            source, vir_held.at[p, j], vir_send.at[p, j], vir_recv.at[p, j], owner, peer_rank
        )

    def pass_vir(p):
        for k in range(1, chips):
            spread[p, 2 * k - 1].wait_recv()
            send_vir(p, k, 1, vir_held.at[p, 2 * k - 1], partner)

    def send_ring(b, source):
        ring[b] = send(
            source, held.at[b - 1], ring_send.at[b - 1], ring_recv.at[b - 1],
            above if b % 2 else below,
        )

    def pass_on(b):
        direct[b, 2].wait_recv()
        passed[b] = send(
            relay.at[b], arrived.at[1, b], pass_send.at[b], pass_recv.at[b],
            before if b % 2 else after,
        )

    def accumulate(p):
        first, second = 2 * p, 2 * p + 1
        for b in (first, second):
            direct[b, 1].wait_recv()
            direct[b, 3].wait_recv()
            passed[b].wait_recv()
        for r in range(ROWS):
            for h in range(batch // 2):
                cols = slice(2 * part * h, 2 * part * (h + 1))
                if r == 0:
                    one, two = own[first, :, cols], own[second, :, cols]
                else:
                    one, two = arrived[r - 1, first, :, cols], arrived[r - 1, second, :, cols]
                place = slice(2 * part * r, 2 * part * (r + 1))
                rows[width * 2 * h : width * (2 * h + 1), place] = jnp.concatenate(
                    [one[:, :part], two[:, :part]], axis=1
                )
                rows[width * (2 * h + 1) : width * (2 * h + 2), place] = jnp.concatenate(
                    [one[:, part:], two[:, part:]], axis=1
                )
        half = rows.shape[0] // 2
        for t in range(2):
            product = lax.dot_general(
                rows[half * t : half * (t + 1)],
                rows[...],
                (((1,), (1,)), ((), ())),
                preferred_element_type=jnp.float32,
            )
            if p == 0:
                gram[half * t : half * (t + 1)] = product
            else:
                gram[half * t : half * (t + 1)] += product

    send_ring(1, half_ref)
    send_ring(2, half_ref)
    for p in range(parts):
        for k in range(1, chips):
            send_vir(p, k, 0, vir_ref.at[p], lax.rem(rank + 2 * k, ranks))
        send_vir(p, 0, 1, vir_ref.at[p], partner)
    pass_vir(0)
    for b in range(blocks):
        if b > 0:
            ring[b].wait_recv()
            if b + 2 < blocks:
                send_ring(b + 2, held.at[b - 1])
        if b % 2 == 0:
            p = b // 2
            for k in range(chips):
                spread[p, 2 * k].wait_recv()
            wide = jnp.concatenate(
                [vir_ref[p]] + [vir_held[p, j] for j in range(ranks - 1)], axis=1
            )
            placed = jnp.dot(
                wide, place_ref[...], preferred_element_type=jnp.float32
            ).astype(jnp.bfloat16)
        t = b % 2
        summed = lax.dot_general(
            placed[:, span * t : span * (t + 1)],
            half_ref[...] if b == 0 else held[b - 1],
            (((0,), (0,)), ((), ())),
            preferred_element_type=jnp.float32,
        ).astype(jnp.bfloat16)
        own[b] = summed[:width]
        for r in range(1, ROWS):
            stage[b, r - 1] = summed[width * r : width * (r + 1)]
        direct[b, 1] = send(
            stage.at[b, 0], arrived.at[0, b], step_send.at[b, 0], step_recv.at[b, 0], after
        )
        direct[b, 3] = send(
            stage.at[b, 2], arrived.at[2, b], step_send.at[b, 2], step_recv.at[b, 2], before
        )
        direct[b, 2] = send(
            stage.at[b, 1], relay.at[b], step_send.at[b, 1], step_recv.at[b, 1],
            before if b % 2 else after,
        )
        if b > 0:
            pass_on(b - 1)
        if b % 2 and (b + 1) // 2 < parts:
            pass_vir((b + 1) // 2)
        if b % 2 and b > 2:
            accumulate((b - 3) // 2)
    pass_on(blocks - 1)
    accumulate(blocks // 2 - 1)

    kept = width // ranks
    for a in range(ranks):
        for i in range(batch):
            sorted_rows[a, kept * i : kept * (i + 1)] = gram[
                width * i + kept * a : width * i + kept * (a + 1)
            ]
    chip = rank // 2
    order = [*range(1, chips), 0]
    for k in order:
        theirs = 2 * lax.rem(chip + k, chips) + 1 - core
        joins[k] = send(
            sorted_rows.at[theirs], joined.at[k], join_send.at[k], join_recv.at[k], owner, partner
        )
    for k in order:
        joins[k].wait_recv()
        both = sorted_rows[2 * lax.rem(chip + k, chips) + core] + joined[k]
        if k > 0:
            mine[k - 1] = both.astype(jnp.bfloat16)
            sums[k] = send(
                mine.at[k - 1], others.at[k - 1], sum_send.at[k - 1], sum_recv.at[k - 1],
                owner, lax.rem(rank + 2 * k, ranks),
            )
    for k in range(1, chips):
        sums[k].wait_recv()
        both += others[k - 1].astype(jnp.float32)
    out_ref[...] = both
    for group in (spread, ring, direct, passed, joins, sums):
        for copy in group.values():
            copy.wait_send()


def pick_kernel(
    mine_ref, index_ref, wanted_ref, vir_ref, left_ref, rows_ref, place_ref,
    held, windows, send_sem, recv_sem, window_sem,
):
    owner, rank = lax.axis_index("aux"), lax.axis_index("occ")
    plane, row = owner // ROWS, owner % ROWS
    ranks, owners = held.shape[0], lax.axis_size("aux")
    blocks, depth, columns = windows.shape
    tall = vir_ref.shape[0] // owners
    reads = []
    for b, shift in enumerate(ring_order(blocks)):
        source = lax.rem(plane + shift + blocks, blocks) * ROWS + row
        for n, low in enumerate(range(0, depth, tall)):
            size = min(tall, depth - low)
            start = pl.multiple_of(lax.rem(source + n, owners) * tall, tall)
            read = pltpu.make_async_copy(
                vir_ref.at[pl.ds(start, size)],
                windows.at[b, pl.ds(low, size)],
                window_sem.at[b, n],
            )
            read.start()
            reads.append(read)

    barrier = pltpu.get_barrier_semaphore()
    peers = [(owner, lax.rem(rank + r, ranks)) for r in range(1, ranks)]
    for peer in peers:
        pl.semaphore_signal(barrier, inc=1, device_id=peer, device_id_type=pl.DeviceIdType.MESH)
    pl.semaphore_wait(barrier, ranks - 1)
    copies = []
    for r in range(1, ranks):
        copy = pltpu.make_async_remote_copy(
            src_ref=mine_ref,
            dst_ref=held.at[r],
            send_sem=send_sem.at[r],
            recv_sem=recv_sem.at[r],
            device_id=peers[r - 1],
            device_id_type=pl.DeviceIdType.MESH,
        )
        copy.start()
        copies.append(copy)
    held[0] = mine_ref[...]

    place_ref[...] = jnp.where(
        lax.broadcasted_iota(jnp.int32, place_ref.shape, 0) == wanted_ref[...], 1.0, 0.0
    ).astype(jnp.bfloat16)
    lanes = rows_ref.shape[2]
    group = columns // owners * ROWS
    source = lax.broadcasted_iota(jnp.int32, (2 * columns, lanes), 0)
    target = lax.broadcasted_iota(jnp.int32, (2 * columns, lanes), 1)
    half = lanes // 2
    within = jnp.where(target < half, target, target - half)
    first = jnp.where(target < half, 0, columns) + plane * group
    hits = (source == first + within) & (within < group)
    choose = jnp.where(hits, 1.0, 0.0).astype(jnp.bfloat16)
    for read in reads:
        read.wait()
    for p in range(blocks // 2):
        pair = jnp.concatenate([windows[2 * p], windows[2 * p + 1]], axis=1)
        rows_ref[p] = jnp.dot(pair, choose, preferred_element_type=jnp.float32).astype(jnp.bfloat16)

    for copy in copies:
        copy.wait_recv()
    each = mine_ref.shape[1] // tall
    pieces = []
    for n in range(3):
        block = lax.rem(owner + n, owners)
        slot = lax.rem(rank - block // each + ranks, ranks)
        low = pl.multiple_of(lax.rem(block, each) * tall, tall)
        pieces.append(held[slot, :, pl.ds(low, tall)])
    near = jnp.concatenate(pieces, axis=1)
    column = lax.broadcasted_iota(jnp.int32, (3 * tall, index_ref.shape[1]), 0)
    named = jnp.where(column == index_ref[...], 1.0, 0.0).astype(jnp.bfloat16)
    left_ref[...] = jnp.dot(near, named, preferred_element_type=jnp.float32).astype(jnp.bfloat16)
    for copy in copies:
        copy.wait_send()


def ring_order(count):
    order = [0]
    for k in range(1, count // 2 + 1):
        order += [-k, k]
    return order[:count]


def slot_of(source, rank, ranks):
    chips = ranks // 2
    return 2 * ((rank // 2 - source // 2 + chips) % chips) + (source + rank) % 2


def on_device(ints, blk_atoms, blk_count, occ_coeff, vir_coeff, batch_ids):
    batch = batch_ids.shape[0]
    slots, block_size = ints.shape[0], ints.shape[1]
    aux_local = ints.shape[3]
    ranks = lax.axis_size("occ")
    group_count = lax.axis_size("aux")
    planes = group_count // ROWS
    owner, rank = lax.axis_index("aux"), lax.axis_index("occ")
    plane, row = owner // ROWS, owner % ROWS
    atom_total = vir_coeff.shape[0] // block_size
    step = atom_total // group_count
    window = 2 * step + 1
    depth = window * block_size
    part = aux_local // ranks
    vir_group = vir_coeff.shape[1] // group_count
    width = vir_group * ranks
    lane = 64

    with jax.named_scope("places"):
        target = jnp.arange(2 * ROWS * width, dtype=jnp.int32)[None, :]
        wanted = (
            slot_of(target // vir_group % ranks, rank, ranks) * (2 * lane)
            + (target // (ROWS * width)) * lane
            + ((target // width + row) % ROWS) * vir_group
            + target % vir_group
        )

    with jax.named_scope("half"):
        picked = jnp.take(occ_coeff, batch_ids, axis=0)
        first = (blk_atoms[:, 0, None] - owner * step + atom_total) % atom_total
        index = first * block_size + jnp.arange(block_size, dtype=jnp.int32)
        vmem = pl.BlockSpec(memory_space=pltpu.VMEM)
        dma = pltpu.SemaphoreType.DMA
        left, vir_rows, place = pl.pallas_call(
            pick_kernel,
            out_shape=[
                jax.ShapeDtypeStruct((batch, slots * block_size), jnp.bfloat16),
                jax.ShapeDtypeStruct((planes // 2, depth, 2 * lane), jnp.bfloat16),
                jax.ShapeDtypeStruct((ranks * 2 * lane, 2 * ROWS * width), jnp.bfloat16),
            ],
            in_specs=[vmem] * 3 + [pl.BlockSpec(memory_space=pl.ANY)],
            out_specs=[vmem] * 3,
            scratch_shapes=[
                pltpu.VMEM((ranks, *picked.shape), jnp.bfloat16),
                pltpu.VMEM((planes, depth, vir_coeff.shape[1]), jnp.bfloat16),
                dma((ranks,)),
                dma((ranks,)),
                dma((planes, 3)),
            ],
            compiler_params=pltpu.CompilerParams(collective_id=1, has_side_effects=True),
        )(picked, index.reshape(1, slots * block_size), wanted, vir_coeff)
        offset = (blk_atoms[:, 1] - owner * step + atom_total) % atom_total
        offset = jnp.where(jnp.arange(slots, dtype=jnp.int32) < blk_count[0], offset, -1)
        offset = jnp.repeat(offset, block_size)
        hits = offset[None, :] == jnp.arange(window, dtype=jnp.int32)[:, None]
        spread = jnp.where(hits[:, None, :], left[None], jnp.bfloat16(0))
        mine = lax.dynamic_slice_in_dim(ints, rank * part, part, 3)
        half = jnp.einsum(
            "wik,knq->wniq",
            spread,
            mine.reshape(slots * block_size, block_size, part),
            preferred_element_type=jnp.float32,
        ).astype(jnp.bfloat16)
        half = half.reshape(depth, batch * part)

    with jax.named_scope("fit"):
        total = batch * width
        kept = total // ranks
        piece = (width, batch * part)
        chips = ranks // 2
        pair_ints = pl.pallas_call(
            exchange_kernel,
            out_shape=jax.ShapeDtypeStruct((kept, total), jnp.float32),
            in_specs=[vmem] * 3,
            out_specs=vmem,
            scratch_shapes=[
                pltpu.VMEM((planes // 2, ranks - 1, depth, 2 * lane), jnp.bfloat16),
                pltpu.VMEM((planes - 1, depth, batch * part), jnp.bfloat16),
                pltpu.VMEM((planes, *piece), jnp.bfloat16),
                pltpu.VMEM((planes, ROWS - 1, *piece), jnp.bfloat16),
                pltpu.VMEM((planes, *piece), jnp.bfloat16),
                pltpu.VMEM((ROWS - 1, planes, *piece), jnp.bfloat16),
                pltpu.VMEM((total, ROWS * 2 * part), jnp.bfloat16),
                pltpu.VMEM((total, total), jnp.float32),
                pltpu.VMEM((ranks, kept, total), jnp.float32),
                pltpu.VMEM((chips, kept, total), jnp.float32),
                pltpu.VMEM((chips - 1, kept, total), jnp.bfloat16),
                pltpu.VMEM((chips - 1, kept, total), jnp.bfloat16),
                dma((planes // 2, ranks - 1)),
                dma((planes // 2, ranks - 1)),
                dma((planes - 1,)),
                dma((planes - 1,)),
                dma((planes, ROWS - 1)),
                dma((planes, ROWS - 1)),
                dma((planes,)),
                dma((planes,)),
                dma((chips,)),
                dma((chips,)),
                dma((chips - 1,)),
                dma((chips - 1,)),
            ],
            compiler_params=pltpu.CompilerParams(collective_id=0, has_side_effects=True),
        )(vir_rows, half, place)
        return pair_ints.reshape(batch, 1, vir_group, batch, width)


def solution(mesh):
    in_specs = (
        P(None, None, None, "aux"),
        P("aux", None),
        P("aux"),
        P(None, "occ"),
        P(None, "occ"),
        P(),
    )
    out_specs = P(None, "aux", "occ", None, None)
    return jax.shard_map(
        on_device, mesh=mesh, in_specs=in_specs, out_specs=out_specs, check_vma=False
    )
```

```python
import jax
import jax.numpy as jnp
from jax import lax
from jax.experimental import pallas as pl
from jax.experimental.pallas import tpu as pltpu
from jax.sharding import PartitionSpec as P

ROWS = 4


def exchange_kernel(
    vir_ref, half_ref, place_ref, out_ref,
    vir_held, held, own, stage, relay, arrived, rows, gram, sorted_rows,
    joined, mine, others,
    vir_send, vir_recv, ring_send, ring_recv, step_send, step_recv, pass_send, pass_recv,
    join_send, join_recv, sum_send, sum_recv,
):
    owner, rank = lax.axis_index("aux"), lax.axis_index("occ")
    plane, row = owner // ROWS, owner % ROWS
    blocks = own.shape[0]
    above, below = lax.rem(plane + 1, blocks) * ROWS + row, lax.rem(plane + blocks - 1, blocks) * ROWS + row
    after = plane * ROWS + lax.rem(row + 1, ROWS)
    before = plane * ROWS + lax.rem(row + ROWS - 1, ROWS)
    parts, ranks = vir_ref.shape[0], vir_held.shape[1] + 1
    chips = ranks // 2
    core = lax.rem(rank, 2)
    partner = rank + 1 - 2 * core
    width, lanes = own.shape[1], own.shape[2]
    batch = gram.shape[0] // width
    part = lanes // batch
    span = ROWS * width

    barrier = pltpu.get_barrier_semaphore()
    near = [(peer, rank) for peer in (above, below, after, before)]
    near += [(owner, partner)] + [(owner, lax.rem(rank + 2 * k, ranks)) for k in range(1, chips)]
    for peer in near:
        pl.semaphore_signal(barrier, inc=1, device_id=peer, device_id_type=pl.DeviceIdType.MESH)
    pl.semaphore_wait(barrier, len(near))

    def send(source, target, send_sem, recv_sem, peer, peer_rank=rank):
        copy = pltpu.make_async_remote_copy(
            src_ref=source,
            dst_ref=target,
            send_sem=send_sem,
            recv_sem=recv_sem,
            device_id=(peer, peer_rank),
            device_id_type=pl.DeviceIdType.MESH,
        )
        copy.start()
        return copy

    ring, direct, passed, spread, joins, sums = {}, {}, {}, {}, {}, {}

    def send_vir(p, k, d, source, peer_rank):
        j = 2 * k + d - 1
        spread[p, j] = send(
            source, vir_held.at[p, j], vir_send.at[p, j], vir_recv.at[p, j], owner, peer_rank
        )

    def pass_vir(p):
        for k in range(1, chips):
            spread[p, 2 * k - 1].wait_recv()
            send_vir(p, k, 1, vir_held.at[p, 2 * k - 1], partner)

    def send_ring(b, source):
        ring[b] = send(
            source, held.at[b - 1], ring_send.at[b - 1], ring_recv.at[b - 1],
            above if b % 2 else below,
        )

    halves = ((0, after), (1, before))
    cut = width // 2

    def send_two_away(b):
        for h, peer in halves:
            some = pl.ds(cut * h, cut)
            direct[b, 2, h] = send(
                stage.at[b, 1, some], relay.at[b, some],
                step_send.at[b, 2 + h], step_recv.at[b, 2 + h], peer,
            )

    def pass_on(b):
        for h, peer in halves:
            some = pl.ds(cut * h, cut)
            direct[b, 2, h].wait_recv()
            passed[b, h] = send(
                relay.at[b, some], arrived.at[1, b, some],
                pass_send.at[b, h], pass_recv.at[b, h], peer,
            )

    def accumulate(p, sources):
        first, second = 2 * p, 2 * p + 1
        for b in (first, second):
            for r in sources:
                if r == 2:
                    passed[b, 0].wait_recv()
                    passed[b, 1].wait_recv()
                elif r > 0:
                    direct[b, r].wait_recv()
        for n, r in enumerate(sources):
            for h in range(batch // 2):
                cols = slice(2 * part * h, 2 * part * (h + 1))
                if r == 0:
                    one, two = own[first, :, cols], own[second, :, cols]
                else:
                    one, two = arrived[r - 1, first, :, cols], arrived[r - 1, second, :, cols]
                place = slice(2 * part * n, 2 * part * (n + 1))
                rows[width * 2 * h : width * (2 * h + 1), place] = jnp.concatenate(
                    [one[:, :part], two[:, :part]], axis=1
                )
                rows[width * (2 * h + 1) : width * (2 * h + 2), place] = jnp.concatenate(
                    [one[:, part:], two[:, part:]], axis=1
                )
        half, used = rows.shape[0] // 2, 2 * part * len(sources)
        for t in range(2):
            product = lax.dot_general(
                rows[half * t : half * (t + 1), :used],
                rows[:, :used],
                (((1,), (1,)), ((), ())),
                preferred_element_type=jnp.float32,
            )
            if p == 0:
                gram[half * t : half * (t + 1)] = product
            else:
                gram[half * t : half * (t + 1)] += product

    send_ring(1, half_ref)
    send_ring(2, half_ref)
    for p in range(parts):
        for k in range(1, chips):
            send_vir(p, k, 0, vir_ref.at[p], lax.rem(rank + 2 * k, ranks))
        send_vir(p, 0, 1, vir_ref.at[p], partner)
    pass_vir(0)
    for b in range(blocks):
        if b > 0:
            ring[b].wait_recv()
            if b + 2 < blocks:
                send_ring(b + 2, held.at[b - 1])
        if b % 2 == 0:
            p = b // 2
            for k in range(chips):
                spread[p, 2 * k].wait_recv()
            wide = jnp.concatenate(
                [vir_ref[p]] + [vir_held[p, j] for j in range(ranks - 1)], axis=1
            )
            placed = jnp.dot(
                wide, place_ref[...], preferred_element_type=jnp.float32
            ).astype(jnp.bfloat16)
        t = b % 2
        summed = lax.dot_general(
            placed[:, span * t : span * (t + 1)],
            half_ref[...] if b == 0 else held[b - 1],
            (((0,), (0,)), ((), ())),
            preferred_element_type=jnp.float32,
        ).astype(jnp.bfloat16)
        own[b] = summed[:width]
        for r in range(1, ROWS):
            stage[b, r - 1] = summed[width * r : width * (r + 1)]
        send_two_away(b)
        direct[b, 1] = send(
            stage.at[b, 0], arrived.at[0, b], step_send.at[b, 0], step_recv.at[b, 0], after
        )
        direct[b, 3] = send(
            stage.at[b, 2], arrived.at[2, b], step_send.at[b, 1], step_recv.at[b, 1], before
        )
        if b > 0:
            pass_on(b - 1)
        if b % 2 and (b + 1) // 2 < parts:
            pass_vir((b + 1) // 2)
        if b % 2 and b > 2:
            accumulate((b - 3) // 2, (0, 1, 3, 2))
    pass_on(blocks - 1)
    accumulate(blocks // 2 - 1, (0, 1, 3))
    accumulate(blocks // 2 - 1, (2,))

    kept = width // ranks
    for a in range(ranks):
        for i in range(batch):
            sorted_rows[a, kept * i : kept * (i + 1)] = gram[
                width * i + kept * a : width * i + kept * (a + 1)
            ]
    chip = rank // 2
    order = [chips // 2, *(k for k in range(1, chips) if k != chips // 2), 0]
    for k in order:
        theirs = 2 * lax.rem(chip + k, chips) + 1 - core
        joins[k] = send(
            sorted_rows.at[theirs], joined.at[k], join_send.at[k], join_recv.at[k], owner, partner
        )
    for k in order:
        joins[k].wait_recv()
        both = sorted_rows[2 * lax.rem(chip + k, chips) + core] + joined[k]
        if k > 0:
            mine[k - 1] = both.astype(jnp.bfloat16)
            sums[k] = send(
                mine.at[k - 1], others.at[k - 1], sum_send.at[k - 1], sum_recv.at[k - 1],
                owner, lax.rem(rank + 2 * k, ranks),
            )
    for k in range(1, chips):
        sums[k].wait_recv()
        both += others[k - 1].astype(jnp.float32)
    out_ref[...] = both
    for group in (spread, ring, direct, passed, joins, sums):
        for copy in group.values():
            copy.wait_send()


def pick_kernel(
    mine_ref, index_ref, wanted_ref, vir_ref, left_ref, rows_ref, place_ref,
    held, windows, send_sem, recv_sem, window_sem,
):
    owner, rank = lax.axis_index("aux"), lax.axis_index("occ")
    plane, row = owner // ROWS, owner % ROWS
    ranks, owners = held.shape[0], lax.axis_size("aux")
    blocks, depth, columns = windows.shape
    tall = vir_ref.shape[0] // owners
    reads = []
    for b, shift in enumerate(ring_order(blocks)):
        source = lax.rem(plane + shift + blocks, blocks) * ROWS + row
        for n, low in enumerate(range(0, depth, tall)):
            size = min(tall, depth - low)
            start = pl.multiple_of(lax.rem(source + n, owners) * tall, tall)
            read = pltpu.make_async_copy(
                vir_ref.at[pl.ds(start, size)],
                windows.at[b, pl.ds(low, size)],
                window_sem.at[b, n],
            )
            read.start()
            reads.append(read)

    barrier = pltpu.get_barrier_semaphore()
    peers = [(owner, lax.rem(rank + r, ranks)) for r in range(1, ranks)]
    for peer in peers:
        pl.semaphore_signal(barrier, inc=1, device_id=peer, device_id_type=pl.DeviceIdType.MESH)
    pl.semaphore_wait(barrier, ranks - 1)
    copies = []
    for r in range(1, ranks):
        copy = pltpu.make_async_remote_copy(
            src_ref=mine_ref,
            dst_ref=held.at[r],
            send_sem=send_sem.at[r],
            recv_sem=recv_sem.at[r],
            device_id=peers[r - 1],
            device_id_type=pl.DeviceIdType.MESH,
        )
        copy.start()
        copies.append(copy)
    held[0] = mine_ref[...]

    place_ref[...] = jnp.where(
        lax.broadcasted_iota(jnp.int32, place_ref.shape, 0) == wanted_ref[...], 1.0, 0.0
    ).astype(jnp.bfloat16)
    lanes = rows_ref.shape[2]
    group = columns // owners * ROWS
    source = lax.broadcasted_iota(jnp.int32, (2 * columns, lanes), 0)
    target = lax.broadcasted_iota(jnp.int32, (2 * columns, lanes), 1)
    half = lanes // 2
    within = jnp.where(target < half, target, target - half)
    first = jnp.where(target < half, 0, columns) + plane * group
    hits = (source == first + within) & (within < group)
    choose = jnp.where(hits, 1.0, 0.0).astype(jnp.bfloat16)
    for read in reads:
        read.wait()
    for p in range(blocks // 2):
        pair = jnp.concatenate([windows[2 * p], windows[2 * p + 1]], axis=1)
        rows_ref[p] = jnp.dot(pair, choose, preferred_element_type=jnp.float32).astype(jnp.bfloat16)

    for copy in copies:
        copy.wait_recv()
    each = mine_ref.shape[1] // tall
    pieces = []
    for n in range(3):
        block = lax.rem(owner + n, owners)
        slot = lax.rem(rank - block // each + ranks, ranks)
        low = pl.multiple_of(lax.rem(block, each) * tall, tall)
        pieces.append(held[slot, :, pl.ds(low, tall)])
    near = jnp.concatenate(pieces, axis=1)
    column = lax.broadcasted_iota(jnp.int32, (3 * tall, index_ref.shape[1]), 0)
    named = jnp.where(column == index_ref[...], 1.0, 0.0).astype(jnp.bfloat16)
    left_ref[...] = jnp.dot(near, named, preferred_element_type=jnp.float32).astype(jnp.bfloat16)
    for copy in copies:
        copy.wait_send()


def ring_order(count):
    order = [0]
    for k in range(1, count // 2 + 1):
        order += [-k, k]
    return order[:count]


def slot_of(source, rank, ranks):
    chips = ranks // 2
    return 2 * ((rank // 2 - source // 2 + chips) % chips) + (source + rank) % 2


def on_device(ints, blk_atoms, blk_count, occ_coeff, vir_coeff, batch_ids):
    batch = batch_ids.shape[0]
    slots, block_size = ints.shape[0], ints.shape[1]
    aux_local = ints.shape[3]
    ranks = lax.axis_size("occ")
    group_count = lax.axis_size("aux")
    planes = group_count // ROWS
    owner, rank = lax.axis_index("aux"), lax.axis_index("occ")
    plane, row = owner // ROWS, owner % ROWS
    atom_total = vir_coeff.shape[0] // block_size
    step = atom_total // group_count
    window = 2 * step + 1
    depth = window * block_size
    part = aux_local // ranks
    vir_group = vir_coeff.shape[1] // group_count
    width = vir_group * ranks
    lane = 64

    with jax.named_scope("places"):
        target = jnp.arange(2 * ROWS * width, dtype=jnp.int32)[None, :]
        wanted = (
            slot_of(target // vir_group % ranks, rank, ranks) * (2 * lane)
            + (target // (ROWS * width)) * lane
            + ((target // width + row) % ROWS) * vir_group
            + target % vir_group
        )

    with jax.named_scope("half"):
        picked = jnp.take(occ_coeff, batch_ids, axis=0)
        first = (blk_atoms[:, 0, None] - owner * step + atom_total) % atom_total
        index = first * block_size + jnp.arange(block_size, dtype=jnp.int32)
        vmem = pl.BlockSpec(memory_space=pltpu.VMEM)
        dma = pltpu.SemaphoreType.DMA
        left, vir_rows, place = pl.pallas_call(
            pick_kernel,
            out_shape=[
                jax.ShapeDtypeStruct((batch, slots * block_size), jnp.bfloat16),
                jax.ShapeDtypeStruct((planes // 2, depth, 2 * lane), jnp.bfloat16),
                jax.ShapeDtypeStruct((ranks * 2 * lane, 2 * ROWS * width), jnp.bfloat16),
            ],
            in_specs=[vmem] * 3 + [pl.BlockSpec(memory_space=pl.ANY)],
            out_specs=[vmem] * 3,
            scratch_shapes=[
                pltpu.VMEM((ranks, *picked.shape), jnp.bfloat16),
                pltpu.VMEM((planes, depth, vir_coeff.shape[1]), jnp.bfloat16),
                dma((ranks,)),
                dma((ranks,)),
                dma((planes, 3)),
            ],
            compiler_params=pltpu.CompilerParams(collective_id=1, has_side_effects=True),
        )(picked, index.reshape(1, slots * block_size), wanted, vir_coeff)
        offset = (blk_atoms[:, 1] - owner * step + atom_total) % atom_total
        offset = jnp.where(jnp.arange(slots, dtype=jnp.int32) < blk_count[0], offset, -1)
        offset = jnp.repeat(offset, block_size)
        hits = offset[None, :] == jnp.arange(window, dtype=jnp.int32)[:, None]
        spread = jnp.where(hits[:, None, :], left[None], jnp.bfloat16(0))
        mine = lax.dynamic_slice_in_dim(ints, rank * part, part, 3)
        half = jnp.einsum(
            "wik,knq->wniq",
            spread,
            mine.reshape(slots * block_size, block_size, part),
            preferred_element_type=jnp.float32,
        ).astype(jnp.bfloat16)
        half = half.reshape(depth, batch * part)

    with jax.named_scope("fit"):
        total = batch * width
        kept = total // ranks
        piece = (width, batch * part)
        chips = ranks // 2
        pair_ints = pl.pallas_call(
            exchange_kernel,
            out_shape=jax.ShapeDtypeStruct((kept, total), jnp.float32),
            in_specs=[vmem] * 3,
            out_specs=vmem,
            scratch_shapes=[
                pltpu.VMEM((planes // 2, ranks - 1, depth, 2 * lane), jnp.bfloat16),
                pltpu.VMEM((planes - 1, depth, batch * part), jnp.bfloat16),
                pltpu.VMEM((planes, *piece), jnp.bfloat16),
                pltpu.VMEM((planes, ROWS - 1, *piece), jnp.bfloat16),
                pltpu.VMEM((planes, *piece), jnp.bfloat16),
                pltpu.VMEM((ROWS - 1, planes, *piece), jnp.bfloat16),
                pltpu.VMEM((total, ROWS * 2 * part), jnp.bfloat16),
                pltpu.VMEM((total, total), jnp.float32),
                pltpu.VMEM((ranks, kept, total), jnp.float32),
                pltpu.VMEM((chips, kept, total), jnp.float32),
                pltpu.VMEM((chips - 1, kept, total), jnp.bfloat16),
                pltpu.VMEM((chips - 1, kept, total), jnp.bfloat16),
                dma((planes // 2, ranks - 1)),
                dma((planes // 2, ranks - 1)),
                dma((planes - 1,)),
                dma((planes - 1,)),
                dma((planes, ROWS)),
                dma((planes, ROWS)),
                dma((planes, 2)),
                dma((planes, 2)),
                dma((chips,)),
                dma((chips,)),
                dma((chips - 1,)),
                dma((chips - 1,)),
            ],
            compiler_params=pltpu.CompilerParams(collective_id=0, has_side_effects=True),
        )(vir_rows, half, place)
        return pair_ints.reshape(batch, 1, vir_group, batch, width)


def solution(mesh):
    in_specs = (
        P(None, None, None, "aux"),
        P("aux", None),
        P("aux"),
        P(None, "occ"),
        P(None, "occ"),
        P(),
    )
    out_specs = P(None, "aux", "occ", None, None)
    return jax.shard_map(
        on_device, mesh=mesh, in_specs=in_specs, out_specs=out_specs, check_vma=False
    )
```

```python
import jax
import jax.numpy as jnp
from jax import lax
from jax.experimental import pallas as pl
from jax.experimental.pallas import tpu as pltpu
from jax.sharding import PartitionSpec as P

ROWS = 4


def exchange_kernel(
    vir_ref, half_ref, place_ref, out_ref,
    vir_held, held, own, stage, relay, arrived, rows, gram, sorted_rows,
    joined, mine, others,
    vir_send, vir_recv, ring_send, ring_recv, step_send, step_recv, pass_send, pass_recv,
    join_send, join_recv, sum_send, sum_recv,
):
    owner, rank = lax.axis_index("aux"), lax.axis_index("occ")
    plane, row = owner // ROWS, owner % ROWS
    blocks = own.shape[0]
    above, below = lax.rem(plane + 1, blocks) * ROWS + row, lax.rem(plane + blocks - 1, blocks) * ROWS + row
    after = plane * ROWS + lax.rem(row + 1, ROWS)
    before = plane * ROWS + lax.rem(row + ROWS - 1, ROWS)
    parts, ranks = vir_ref.shape[0], vir_held.shape[1] + 1
    chips = ranks // 2
    core = lax.rem(rank, 2)
    partner = rank + 1 - 2 * core
    width, lanes = own.shape[1], own.shape[2]
    batch = gram.shape[0] // width
    part = lanes // batch
    span = ROWS * width

    barrier = pltpu.get_barrier_semaphore()
    near = [(peer, rank) for peer in (above, below, after, before)]
    near += [(owner, partner)] + [(owner, lax.rem(rank + 2 * k, ranks)) for k in range(1, chips)]
    for peer in near:
        pl.semaphore_signal(barrier, inc=1, device_id=peer, device_id_type=pl.DeviceIdType.MESH)
    pl.semaphore_wait(barrier, len(near))

    def send(source, target, send_sem, recv_sem, peer, peer_rank=rank):
        copy = pltpu.make_async_remote_copy(
            src_ref=source,
            dst_ref=target,
            send_sem=send_sem,
            recv_sem=recv_sem,
            device_id=(peer, peer_rank),
            device_id_type=pl.DeviceIdType.MESH,
        )
        copy.start()
        return copy

    ring, direct, passed, spread, joins, sums = {}, {}, {}, {}, {}, {}

    def send_vir(p, k, d, source, peer_rank):
        j = 2 * k + d - 1
        spread[p, j] = send(
            source, vir_held.at[p, j], vir_send.at[p, j], vir_recv.at[p, j], owner, peer_rank
        )

    def pass_vir(p):
        for k in range(1, chips):
            spread[p, 2 * k - 1].wait_recv()
            send_vir(p, k, 1, vir_held.at[p, 2 * k - 1], partner)

    def send_ring(b, source):
        ring[b] = send(
            source, held.at[b - 1], ring_send.at[b - 1], ring_recv.at[b - 1],
            above if b % 2 else below,
        )

    halves = ((0, after), (1, before))
    cut = width // 2

    def send_two_away(b):
        for h, peer in halves:
            some = pl.ds(cut * h, cut)
            direct[b, 2, h] = send(
                stage.at[b, 1, some], relay.at[b, some],
                step_send.at[b, 2 + h], step_recv.at[b, 2 + h], peer,
            )

    def pass_on(b):
        for h, peer in halves:
            some = pl.ds(cut * h, cut)
            direct[b, 2, h].wait_recv()
            passed[b, h] = send(
                relay.at[b, some], arrived.at[1, b, some],
                pass_send.at[b, h], pass_recv.at[b, h], peer,
            )

    def accumulate(p, sources):
        first, second = 2 * p, 2 * p + 1
        for b in (first, second):
            for r in sources:
                if r == 2:
                    passed[b, 0].wait_recv()
                    passed[b, 1].wait_recv()
                elif r > 0:
                    direct[b, r].wait_recv()
        for n, r in enumerate(sources):
            for h in range(batch // 2):
                cols = slice(2 * part * h, 2 * part * (h + 1))
                if r == 0:
                    one, two = own[first, :, cols], own[second, :, cols]
                else:
                    one, two = arrived[r - 1, first, :, cols], arrived[r - 1, second, :, cols]
                place = slice(2 * part * n, 2 * part * (n + 1))
                rows[width * 2 * h : width * (2 * h + 1), place] = jnp.concatenate(
                    [one[:, :part], two[:, :part]], axis=1
                )
                rows[width * (2 * h + 1) : width * (2 * h + 2), place] = jnp.concatenate(
                    [one[:, part:], two[:, part:]], axis=1
                )
        half, used = rows.shape[0] // 2, 2 * part * len(sources)
        for t in range(2):
            product = lax.dot_general(
                rows[half * t : half * (t + 1), :used],
                rows[:, :used],
                (((1,), (1,)), ((), ())),
                preferred_element_type=jnp.float32,
            )
            if p == 0:
                gram[half * t : half * (t + 1)] = product
            else:
                gram[half * t : half * (t + 1)] += product

    send_ring(1, half_ref)
    send_ring(2, half_ref)
    for p in range(parts):
        for k in range(1, chips):
            send_vir(p, k, 0, vir_ref.at[p], lax.rem(rank + 2 * k, ranks))
        send_vir(p, 0, 1, vir_ref.at[p], partner)
    pass_vir(0)
    for b in range(blocks):
        for c in range(b, min(b + 2, blocks)) if b % 2 else ():
            ring[c].wait_recv()
            if c + 2 < blocks:
                send_ring(c + 2, held.at[c - 1])
        if b % 2 == 0:
            p = b // 2
            for k in range(chips):
                spread[p, 2 * k].wait_recv()
            wide = jnp.concatenate(
                [vir_ref[p]] + [vir_held[p, j] for j in range(ranks - 1)], axis=1
            )
            placed = jnp.dot(
                wide, place_ref[...], preferred_element_type=jnp.float32
            ).astype(jnp.bfloat16)
        t = b % 2
        summed = lax.dot_general(
            placed[:, span * t : span * (t + 1)],
            half_ref[...] if b == 0 else held[b - 1],
            (((0,), (0,)), ((), ())),
            preferred_element_type=jnp.float32,
        ).astype(jnp.bfloat16)
        own[b] = summed[:width]
        for r in range(1, ROWS):
            stage[b, r - 1] = summed[width * r : width * (r + 1)]
        send_two_away(b)
        direct[b, 1] = send(
            stage.at[b, 0], arrived.at[0, b], step_send.at[b, 0], step_recv.at[b, 0], after
        )
        direct[b, 3] = send(
            stage.at[b, 2], arrived.at[2, b], step_send.at[b, 1], step_recv.at[b, 1], before
        )
        if b > 0:
            pass_on(b - 1)
        if b % 2 and (b + 1) // 2 < parts:
            pass_vir((b + 1) // 2)
        if b % 2 and b > 2:
            accumulate((b - 3) // 2, (0, 1, 3, 2))
    pass_on(blocks - 1)
    accumulate(blocks // 2 - 1, (0, 1, 3))
    accumulate(blocks // 2 - 1, (2,))

    kept = width // ranks
    for a in range(ranks):
        for i in range(batch):
            sorted_rows[a, kept * i : kept * (i + 1)] = gram[
                width * i + kept * a : width * i + kept * (a + 1)
            ]
    chip = rank // 2
    order = [chips // 2, *(k for k in range(1, chips) if k != chips // 2), 0]
    for k in order:
        theirs = 2 * lax.rem(chip + k, chips) + 1 - core
        joins[k] = send(
            sorted_rows.at[theirs], joined.at[k], join_send.at[k], join_recv.at[k], owner, partner
        )
    for k in order:
        joins[k].wait_recv()
        both = sorted_rows[2 * lax.rem(chip + k, chips) + core] + joined[k]
        if k > 0:
            mine[k - 1] = both.astype(jnp.bfloat16)
            sums[k] = send(
                mine.at[k - 1], others.at[k - 1], sum_send.at[k - 1], sum_recv.at[k - 1],
                owner, lax.rem(rank + 2 * k, ranks),
            )
    for k in range(1, chips):
        sums[k].wait_recv()
        both += others[k - 1].astype(jnp.float32)
    out_ref[...] = both
    for group in (spread, ring, direct, passed, joins, sums):
        for copy in group.values():
            copy.wait_send()


def pick_kernel(
    mine_ref, index_ref, wanted_ref, vir_ref, left_ref, rows_ref, place_ref,
    held, windows, send_sem, recv_sem, window_sem,
):
    owner, rank = lax.axis_index("aux"), lax.axis_index("occ")
    plane, row = owner // ROWS, owner % ROWS
    ranks, owners = held.shape[0], lax.axis_size("aux")
    blocks, depth, columns = windows.shape
    tall = vir_ref.shape[0] // owners
    reads = []
    for b, shift in enumerate(ring_order(blocks)):
        source = lax.rem(plane + shift + blocks, blocks) * ROWS + row
        for n, low in enumerate(range(0, depth, tall)):
            size = min(tall, depth - low)
            start = pl.multiple_of(lax.rem(source + n, owners) * tall, tall)
            read = pltpu.make_async_copy(
                vir_ref.at[pl.ds(start, size)],
                windows.at[b, pl.ds(low, size)],
                window_sem.at[b, n],
            )
            read.start()
            reads.append(read)

    barrier = pltpu.get_barrier_semaphore()
    peers = [(owner, lax.rem(rank + r, ranks)) for r in range(1, ranks)]
    for peer in peers:
        pl.semaphore_signal(barrier, inc=1, device_id=peer, device_id_type=pl.DeviceIdType.MESH)
    pl.semaphore_wait(barrier, ranks - 1)
    copies = []
    for r in range(1, ranks):
        copy = pltpu.make_async_remote_copy(
            src_ref=mine_ref,
            dst_ref=held.at[r],
            send_sem=send_sem.at[r],
            recv_sem=recv_sem.at[r],
            device_id=peers[r - 1],
            device_id_type=pl.DeviceIdType.MESH,
        )
        copy.start()
        copies.append(copy)
    held[0] = mine_ref[...]

    place_ref[...] = jnp.where(
        lax.broadcasted_iota(jnp.int32, place_ref.shape, 0) == wanted_ref[...], 1.0, 0.0
    ).astype(jnp.bfloat16)
    lanes = rows_ref.shape[2]
    group = columns // owners * ROWS
    source = lax.broadcasted_iota(jnp.int32, (2 * columns, lanes), 0)
    target = lax.broadcasted_iota(jnp.int32, (2 * columns, lanes), 1)
    half = lanes // 2
    within = jnp.where(target < half, target, target - half)
    first = jnp.where(target < half, 0, columns) + plane * group
    hits = (source == first + within) & (within < group)
    choose = jnp.where(hits, 1.0, 0.0).astype(jnp.bfloat16)
    for read in reads:
        read.wait()
    for p in range(blocks // 2):
        pair = jnp.concatenate([windows[2 * p], windows[2 * p + 1]], axis=1)
        rows_ref[p] = jnp.dot(pair, choose, preferred_element_type=jnp.float32).astype(jnp.bfloat16)

    for copy in copies:
        copy.wait_recv()
    each = mine_ref.shape[1] // tall
    pieces = []
    for n in range(3):
        block = lax.rem(owner + n, owners)
        slot = lax.rem(rank - block // each + ranks, ranks)
        low = pl.multiple_of(lax.rem(block, each) * tall, tall)
        pieces.append(held[slot, :, pl.ds(low, tall)])
    near = jnp.concatenate(pieces, axis=1)
    column = lax.broadcasted_iota(jnp.int32, (3 * tall, index_ref.shape[1]), 0)
    named = jnp.where(column == index_ref[...], 1.0, 0.0).astype(jnp.bfloat16)
    left_ref[...] = jnp.dot(near, named, preferred_element_type=jnp.float32).astype(jnp.bfloat16)
    for copy in copies:
        copy.wait_send()


def ring_order(count):
    order = [0]
    for k in range(1, count // 2 + 1):
        order += [-k, k]
    return order[:count]


def slot_of(source, rank, ranks):
    chips = ranks // 2
    return 2 * ((rank // 2 - source // 2 + chips) % chips) + (source + rank) % 2


def on_device(ints, blk_atoms, blk_count, occ_coeff, vir_coeff, batch_ids):
    batch = batch_ids.shape[0]
    slots, block_size = ints.shape[0], ints.shape[1]
    aux_local = ints.shape[3]
    ranks = lax.axis_size("occ")
    group_count = lax.axis_size("aux")
    planes = group_count // ROWS
    owner, rank = lax.axis_index("aux"), lax.axis_index("occ")
    plane, row = owner // ROWS, owner % ROWS
    atom_total = vir_coeff.shape[0] // block_size
    step = atom_total // group_count
    window = 2 * step + 1
    depth = window * block_size
    part = aux_local // ranks
    vir_group = vir_coeff.shape[1] // group_count
    width = vir_group * ranks
    lane = 64

    with jax.named_scope("places"):
        target = jnp.arange(2 * ROWS * width, dtype=jnp.int32)[None, :]
        wanted = (
            slot_of(target // vir_group % ranks, rank, ranks) * (2 * lane)
            + (target // (ROWS * width)) * lane
            + ((target // width + row) % ROWS) * vir_group
            + target % vir_group
        )

    with jax.named_scope("half"):
        picked = jnp.take(occ_coeff, batch_ids, axis=0)
        first = (blk_atoms[:, 0, None] - owner * step + atom_total) % atom_total
        index = first * block_size + jnp.arange(block_size, dtype=jnp.int32)
        vmem = pl.BlockSpec(memory_space=pltpu.VMEM)
        dma = pltpu.SemaphoreType.DMA
        left, vir_rows, place = pl.pallas_call(
            pick_kernel,
            out_shape=[
                jax.ShapeDtypeStruct((batch, slots * block_size), jnp.bfloat16),
                jax.ShapeDtypeStruct((planes // 2, depth, 2 * lane), jnp.bfloat16),
                jax.ShapeDtypeStruct((ranks * 2 * lane, 2 * ROWS * width), jnp.bfloat16),
            ],
            in_specs=[vmem] * 3 + [pl.BlockSpec(memory_space=pl.ANY)],
            out_specs=[vmem] * 3,
            scratch_shapes=[
                pltpu.VMEM((ranks, *picked.shape), jnp.bfloat16),
                pltpu.VMEM((planes, depth, vir_coeff.shape[1]), jnp.bfloat16),
                dma((ranks,)),
                dma((ranks,)),
                dma((planes, 3)),
            ],
            compiler_params=pltpu.CompilerParams(collective_id=1, has_side_effects=True),
        )(picked, index.reshape(1, slots * block_size), wanted, vir_coeff)
        offset = (blk_atoms[:, 1] - owner * step + atom_total) % atom_total
        offset = jnp.where(jnp.arange(slots, dtype=jnp.int32) < blk_count[0], offset, -1)
        offset = jnp.repeat(offset, block_size)
        hits = offset[None, :] == jnp.arange(window, dtype=jnp.int32)[:, None]
        spread = jnp.where(hits[:, None, :], left[None], jnp.bfloat16(0))
        mine = lax.dynamic_slice_in_dim(ints, rank * part, part, 3)
        half = jnp.einsum(
            "wik,knq->wniq",
            spread,
            mine.reshape(slots * block_size, block_size, part),
            preferred_element_type=jnp.float32,
        ).astype(jnp.bfloat16)
        half = half.reshape(depth, batch * part)

    with jax.named_scope("fit"):
        total = batch * width
        kept = total // ranks
        piece = (width, batch * part)
        chips = ranks // 2
        pair_ints = pl.pallas_call(
            exchange_kernel,
            out_shape=jax.ShapeDtypeStruct((kept, total), jnp.float32),
            in_specs=[vmem] * 3,
            out_specs=vmem,
            scratch_shapes=[
                pltpu.VMEM((planes // 2, ranks - 1, depth, 2 * lane), jnp.bfloat16),
                pltpu.VMEM((planes - 1, depth, batch * part), jnp.bfloat16),
                pltpu.VMEM((planes, *piece), jnp.bfloat16),
                pltpu.VMEM((planes, ROWS - 1, *piece), jnp.bfloat16),
                pltpu.VMEM((planes, *piece), jnp.bfloat16),
                pltpu.VMEM((ROWS - 1, planes, *piece), jnp.bfloat16),
                pltpu.VMEM((total, ROWS * 2 * part), jnp.bfloat16),
                pltpu.VMEM((total, total), jnp.float32),
                pltpu.VMEM((ranks, kept, total), jnp.float32),
                pltpu.VMEM((chips, kept, total), jnp.float32),
                pltpu.VMEM((chips - 1, kept, total), jnp.bfloat16),
                pltpu.VMEM((chips - 1, kept, total), jnp.bfloat16),
                dma((planes // 2, ranks - 1)),
                dma((planes // 2, ranks - 1)),
                dma((planes - 1,)),
                dma((planes - 1,)),
                dma((planes, ROWS)),
                dma((planes, ROWS)),
                dma((planes, 2)),
                dma((planes, 2)),
                dma((chips,)),
                dma((chips,)),
                dma((chips - 1,)),
                dma((chips - 1,)),
            ],
            compiler_params=pltpu.CompilerParams(collective_id=0, has_side_effects=True),
        )(vir_rows, half, place)
        return pair_ints.reshape(batch, 1, vir_group, batch, width)


def solution(mesh):
    in_specs = (
        P(None, None, None, "aux"),
        P("aux", None),
        P("aux"),
        P(None, "occ"),
        P(None, "occ"),
        P(),
    )
    out_specs = P(None, "aux", "occ", None, None)
    return jax.shard_map(
        on_device, mesh=mesh, in_specs=in_specs, out_specs=out_specs, check_vma=False
    )
```
